32 devices in a mesh: pairs: 2 (over x), src: 8 (over z, y), tgt: 2 (over core).
Axes of the slice: x: 2, y: 2, z: 4, core: 2. Of those that a mesh axis runs over, the one named last changes fastest.
Arguments:
- src_feat: float32 [2048, 32], P(('pairs', 'src'), 'tgt'), parts along dimension 0, may hold values from -0.72 to 0.72
- tgt_feat: float32 [32768, 32], P(('pairs', 'tgt'), 'src'), parts along dimension 0, may hold values from -0.72 to 0.72
- tgt_dual: float32 [32768], P(('pairs', 'tgt')), parts along dimension 0, may hold values from -6 to 6
- core_matrix: float32 [68, 34], P('pairs'), parts along dimension 0, may hold values from -3 to 3
Outputs:
- src_dual: float32 [2048], P(('pairs', 'src')), parts along dimension 0
- tgt_dual_out: float32 [32768], P(('pairs', 'tgt')), parts along dimension 0
- core_out: float32 [68, 34], P('pairs'), parts along dimension 0
The draws below stay inside these ranges and needn't reach their ends.
There are 2 independent parts, one for each index of `pairs`. The reference program is written for one: setup_inputs(seed, part) draws one part's arguments, and reference() takes and returns one part's arrays. A program takes and returns all parts, laid end to end along the dimension named above; each array names one. Nothing has to cross between parts.
All inputs are finite; a program needn't handle non-finite values.
Results may differ from the reference program's by a relative error of at most 0.0003.
Values sent between devices are 32-bit elements; how exact they have to be, the bound alone decides.
No kernel may reach another device: no remote copies, remote signals or barrier semaphores. Data moves between devices by JAX's collectives and lax.ppermute only.
A program may use at most 64 MiB of HBM per device.

```python
import jax
import jax.numpy as jnp
from jax import lax

FEAT = 32
RANK = 34
RS = 128
OUTER = 2
NS = 1024
NT = 16384


def block_levels(rng, dims, cuts, smallest, largest):
    level = 1.0
    for dim, shards_of in cuts:
        steps = jax.random.uniform(jax.random.fold_in(jax.random.fold_in(rng, 6), dim), (shards_of,), jnp.float32, smallest / len(cuts), largest / len(cuts))
        level = level * jnp.repeat(jnp.exp(steps), dims[dim] // shards_of).reshape((-1,) + (1,) * (len(dims) - 1 - dim))
    return level


def bell_draw(stream_key, dims, scale, reach, split=(), dtype=jnp.bfloat16):
    array = scale * jax.random.normal(stream_key, dims, jnp.float32)
    if split:
        array = array * block_levels(stream_key, dims, split, -0.22, 0.18)
    return jnp.clip(array, -reach, reach).astype(dtype)


def setup_inputs(seed: int = 0, part: int = 0) -> dict:
    seeds = jax.random.split(jax.random.key(seed), 5)
    own_keys = jax.random.split(jax.random.fold_in(seeds[4], part), 5)
    return {
        "src_feat": bell_draw(own_keys[0], (NS, FEAT), 0.12, 0.72, ((0, 8), (1, 2)), jnp.float32),
        "tgt_feat": bell_draw(own_keys[1], (NT, FEAT), 0.12, 0.72, ((0, 2), (1, 8)), jnp.float32),
        "tgt_dual": bell_draw(own_keys[2], (NT,), 1.0, 6.0, ((0, 2),), jnp.float32),
        "core_matrix": bell_draw(own_keys[3], (RANK, RANK), 0.5, 3.0, (), jnp.float32),
    }


EPSILON = 0.02
HIGH = lax.Precision.HIGHEST


def lifted(values):
    squares = jnp.sum(values * values, axis=1, keepdims=True)
    ones = jnp.ones_like(squares)
    left = jnp.concatenate([squares, ones, -2.0 * values], axis=1)
    right = jnp.concatenate([ones, squares, values], axis=1)
    return left, right


def merge_logsum(earlier, later):
    top = jnp.maximum(earlier[0], later[0])
    return (top, earlier[1] * jnp.exp(earlier[0] - top) + later[1] * jnp.exp(later[0] - top))


def reference(src_feat, tgt_feat, tgt_dual, core_matrix):
    src_left, src_right = lifted(src_feat)
    tgt_left, tgt_right = lifted(tgt_feat)
    log_src = -jnp.log(jnp.float32(NS))
    log_tgt = -jnp.log(jnp.float32(NT))
    blocks = NS // RS
    right_blocks = src_right.reshape(blocks, RS, RANK)
    src_dual = jnp.zeros((NS,), jnp.float32)
    for outer_step in range(OUTER):
        projected = jnp.dot(src_left, core_matrix, precision=HIGH).reshape(blocks, RS, RANK)

        def row_block(proj):
            linear = jnp.dot(proj, tgt_right.T, precision=HIGH)
            logits = (tgt_dual[None, :] - linear) / EPSILON
            top = jnp.max(logits, axis=1)
            total = jnp.sum(jnp.exp(logits - top[:, None]), axis=1)
            return EPSILON * log_src - EPSILON * (top + jnp.log(total))

        src_dual = lax.map(row_block, projected).reshape(NS)
        dual_blocks = src_dual.reshape(blocks, RS)

        def col_block(carry, inputs):
            proj, duals = inputs
            linear = jnp.dot(proj, tgt_right.T, precision=HIGH)
            logits = (duals[:, None] - linear) / EPSILON
            top = jnp.max(logits, axis=0)
            total = jnp.sum(jnp.exp(logits - top[None, :]), axis=0)
            return merge_logsum(carry, (top, total)), None

        start = (jnp.full((NT,), -jnp.inf, jnp.float32), jnp.zeros((NT,), jnp.float32))
        (top, total), unused = lax.scan(col_block, start, (projected, dual_blocks))
        tgt_dual = EPSILON * log_tgt - EPSILON * (top + jnp.log(total))

        def core_block(carry, inputs):
            proj, duals, right = inputs
            linear = jnp.dot(proj, tgt_right.T, precision=HIGH)
            coupling = jnp.exp((duals[:, None] + tgt_dual[None, :] - linear) / EPSILON)
            weighted = jnp.dot(coupling, tgt_left, precision=HIGH)
            return carry + jnp.dot(right.T, weighted, precision=HIGH), None

        core_sum, unused = lax.scan(core_block, jnp.zeros((RANK, RANK), jnp.float32),
                                    (projected, dual_blocks, right_blocks))
        core_matrix = -2.0 * core_sum
    return src_dual, tgt_dual, core_matrix
```

```python
import functools
import math

import jax
import jax.numpy as jnp
from jax import lax
from jax.experimental import pallas as pl
from jax.experimental.pallas import tpu as pltpu
from jax.sharding import PartitionSpec as P

OUTER = 2
EPSILON = 0.02
SCALE = math.log2(math.e) / EPSILON
HIGH = lax.Precision.HIGHEST
F32 = jnp.float32
BF16 = jnp.bfloat16
FEAT = 32
RANKS = FEAT + 2
PAD = 40
WIDE = 48
DEPTH = 256
LANES = 128
SHIFT = 42
GROUP = 16
CHUNK = 256
NT_DIMS = (((1,), (1,)), ((), ()))


def thirds(values):
    first = values.astype(BF16).astype(F32)
    rest = values - first
    second = rest.astype(BF16).astype(F32)
    third = (rest - second).astype(BF16).astype(F32)
    return first, second, third


def left_order(parts):
    return [parts[0], parts[0], parts[1], parts[0], parts[1], parts[2]]


def right_order(parts):
    return [parts[0], parts[1], parts[0], parts[2], parts[1], parts[0]]


def stacked(rows, count):
    width = rows[0].shape[1]
    index = lax.broadcasted_iota(jnp.int32, (count, width), 0)
    out = jnp.zeros((count, width), F32)
    for k, row in enumerate(rows):
        out = jnp.where(index == k, jnp.broadcast_to(row, (count, width)), out)
    return out


def packed(core_ref, core):
    core_ref[...] = jnp.zeros_like(core_ref)
    core_ref[: core.shape[0], : core.shape[1]] = core
    return (
        core_ref[0:GROUP]
        + pltpu.roll(core_ref[GROUP : 2 * GROUP], SHIFT, 1)
        + pltpu.roll(core_ref[2 * GROUP : 3 * GROUP], 2 * SHIFT, 1)
    )


def unpacked(block):
    pieces = [block, pltpu.roll(block, LANES - SHIFT, 1), pltpu.roll(block, LANES - 2 * SHIFT, 1)]
    whole = jnp.concatenate(pieces, axis=0)
    lane = lax.broadcasted_iota(jnp.int32, whole.shape, 1)
    return jnp.where(lane < RANKS, whole, 0.0)


def row_of(blocks):
    return jnp.concatenate([blocks[k : k + 1] for k in range(blocks.shape[0])], axis=1)


def extras(cross, fixed, ones):
    rows = left_order(thirds(cross)) + list(thirds(fixed))
    if ones:
        rows += [jnp.ones_like(fixed)] * 3
    block = stacked(rows, 16).astype(BF16)
    return jnp.concatenate([block, jnp.zeros((DEPTH - 6 * FEAT - 16, block.shape[1]), BF16)], axis=0)


def row_pass(core, scale, left, right_ref, main_ref, tail_ref, part_ref):
    proj = scale * jnp.dot(core, left, precision=HIGH, preferred_element_type=F32)
    main = jnp.concatenate(left_order(thirds(proj[:FEAT])), axis=0).astype(BF16)
    main_ref[...] = main
    tail_ref[...] = proj[FEAT:PAD]
    weights = jnp.concatenate([main, extras(proj[FEAT + 1 : FEAT + 2], proj[FEAT : FEAT + 1], True)], axis=0)
    count = right_ref.shape[0]
    size = min(CHUNK, count)
    top = total = None
    for start in range(0, count, size):
        logits = jnp.dot(right_ref[start : start + size], weights, preferred_element_type=F32)
        high = jnp.max(logits, axis=0, keepdims=True)
        if top is None:
            top = high
            total = jnp.sum(jnp.exp2(logits - top), axis=0, keepdims=True)
        else:
            new = jnp.maximum(top, high)
            total = total * jnp.exp2(top - new) + jnp.sum(jnp.exp2(logits - new), axis=0, keepdims=True)
            top = new
    part = top + jnp.log2(total)
    peers, blocks, lanes = part_ref.shape
    for k in range(blocks):
        piece = part[:, k * lanes : (k + 1) * lanes]
        for peer in range(peers):
            part_ref[peer, k : k + 1, :] = piece


def first_rows(halves, src_ref, tgt_ref, dual_ref, core_ref, left_ref, tgtl_ref, right_ref, main_ref, tail_ref, part_ref):
    peers = src_ref.shape[0]
    columns = []
    for start in range(0, peers, halves):
        columns.append(jnp.concatenate([src_ref[start + t] for t in range(halves)], axis=0))
    src = jnp.concatenate(columns, axis=1)
    squares = jnp.sum(src * src, axis=0, keepdims=True)
    left_ref[0:FEAT] = -2.0 * src
    left_ref[FEAT:PAD] = stacked([jnp.ones_like(squares), squares], PAD - FEAT)

    blocks, feats, count = tgt_ref.shape
    for k in range(blocks):
        tgtl_ref[k * feats : (k + 1) * feats] = tgt_ref[k]
    tgt = tgtl_ref[0:FEAT]
    norms = jnp.sum(tgt * tgt, axis=0, keepdims=True)
    tgtl_ref[0:FEAT] = -2.0 * tgt
    tgtl_ref[FEAT:PAD] = stacked([norms, jnp.ones_like(norms)], PAD - FEAT)
    start = pl.multiple_of(lax.axis_index("src") * count, LANES)
    dual = SCALE * dual_ref[:, pl.ds(start, count)]
    rows = right_order(thirds(norms)) + [jnp.ones_like(norms)] * 3 + list(thirds(dual))
    tail = jnp.concatenate([stacked(rows, 16), jnp.zeros((DEPTH - 6 * FEAT - 16, count), F32)], axis=0)
    right = jnp.concatenate(right_order(thirds(tgt)) + [tail], axis=0)
    right_ref[...] = right.T.astype(BF16)
    row_pass(core_ref[...], -SCALE, left_ref[...], right_ref, main_ref, tail_ref, part_ref)


def later_rows(core_ref, left_ref, right_ref, main_ref, tail_ref, part_ref):
    core = unpacked(jnp.sum(core_ref[...], axis=0))
    row_pass(core[:PAD, :PAD], 2.0 * SCALE, left_ref[...], right_ref, main_ref, tail_ref, part_ref)


def fold_dual(dual_ref, right_ref, out_ref):
    out_ref[...] = right_ref[...]
    for k in range(dual_ref.shape[0]):
        dual = jnp.broadcast_to(dual_ref[k : k + 1], (LANES, LANES)).T
        parts = thirds(dual)
        old = right_ref[k * LANES : (k + 1) * LANES, LANES:].astype(F32)
        lane = lax.broadcasted_iota(jnp.int32, old.shape, 1) - (6 * FEAT + 9 - LANES)
        for t in range(3):
            old = jnp.where(lane == t, parts[t], old)
        out_ref[k * LANES : (k + 1) * LANES, LANES:] = old.astype(BF16)


def col_pass(sizes, part_ref, main_ref, tail_ref, right_ref, left_ref, tgtl_ref, own_ref, dual_ref, out_ref, pack_ref):
    src_total, tgt_total = sizes
    parts = part_ref[...]
    top = jnp.max(parts, axis=0)
    summed = top + jnp.log2(jnp.sum(jnp.exp2(parts - top[None]), axis=0))
    src_dual = -math.log2(src_total) - summed
    own_rows = own_ref.shape[0]
    pack_ref[0 : src_dual.shape[0]] = src_dual
    own_ref[...] = pack_ref[pl.ds(lax.axis_index("src") * own_rows, own_rows)] * (1.0 / SCALE)

    tail = extras(tail_ref[1:2], tail_ref[0:1] + row_of(src_dual), False)
    weights = jnp.concatenate([main_ref[...], tail], axis=0)
    src = -0.5 * left_ref[0:FEAT]
    squares = left_ref[FEAT + 1 : FEAT + 2]
    ones = left_ref[FEAT : FEAT + 1]
    feats = thirds(src)
    norms = thirds(squares)
    factors = jnp.concatenate(
        [feats[0], stacked([norms[0], ones], GROUP), feats[1], stacked([norms[1]], GROUP)], axis=0
    ).astype(BF16)
    count = right_ref.shape[0]
    size = min(CHUNK, count)
    row = lax.broadcasted_iota(jnp.int32, (LANES, LANES), 0)
    eye = row == lax.broadcasted_iota(jnp.int32, (LANES, LANES), 1)
    core = jnp.zeros((PAD, WIDE), F32)
    peers = out_ref.shape[0]
    for start in range(0, count, size):
        logits = jnp.dot(right_ref[start : start + size], weights, preferred_element_type=F32)
        high = jnp.max(logits, axis=1, keepdims=True)
        weight = jnp.exp2(logits - high)
        coarse = weight.astype(BF16)
        fine = (weight - coarse.astype(F32)).astype(BF16)
        both = lax.dot_general(factors, coarse, NT_DIMS, preferred_element_type=F32)
        rest = lax.dot_general(factors[:WIDE], fine, NT_DIMS, preferred_element_type=F32)
        moments = both[:WIDE] + both[WIDE:] + rest
        total = moments[FEAT + 1 : FEAT + 2]
        tops = []
        for k in range(0, size, LANES):
            block = jnp.broadcast_to(high[k : k + LANES], (LANES, LANES))
            tops.append(jnp.sum(jnp.where(eye, block, 0.0), axis=0, keepdims=True))
        tops = jnp.concatenate(tops, axis=1)
        dual = -math.log2(tgt_total) - (tops + jnp.log2(total))
        for k in range(0, size, LANES):
            dual_ref[(start + k) // LANES : (start + k) // LANES + 1] = dual[:, k : k + LANES]
        moments = moments * ((1.0 / tgt_total) / total)
        core = core + lax.dot_general(
            tgtl_ref[:, start : start + size], moments, NT_DIMS, precision=HIGH, preferred_element_type=F32
        )
    block = packed(pack_ref, core)
    for peer in range(peers):
        out_ref[peer, 0:GROUP] = block
    if out_ref.shape[1] > GROUP:
        for peer in range(peers):
            out_ref[peer, GROUP:] = dual_ref[...]


def finish(halves, in_ref, dual_ref, core_ref):
    half = lax.axis_index("tgt")
    for k in range(dual_ref.shape[0]):
        dual_ref[k] = in_ref[k * halves + half, GROUP:] * (1.0 / SCALE)
    core = unpacked(jnp.sum(in_ref[:, 0:GROUP], axis=0))
    core = jnp.concatenate([core[FEAT:RANKS], core[:FEAT], jnp.zeros((LANES - RANKS, LANES), F32)], axis=0)
    lane = lax.broadcasted_iota(jnp.int32, core.shape, 1)
    moved = pltpu.roll(core, 2, 1)
    moved = jnp.where(lane == 0, pltpu.roll(core, LANES - FEAT - 1, 1), moved)
    moved = jnp.where(lane == 1, pltpu.roll(core, LANES - FEAT + 1, 1), moved)
    core_ref[...] = -2.0 * moved.T[:RANKS, :RANKS]


def call(body, outs, *args, scratch=()):
    spec = pl.BlockSpec(memory_space=pltpu.VMEM)
    return pl.pallas_call(
        body,
        out_shape=[jax.ShapeDtypeStruct(shape, dtype) for shape, dtype in outs],
        in_specs=[spec] * len(args),
        out_specs=[spec] * len(outs),
        scratch_shapes=scratch,
    )(*args)


def exchanged(blocks, axes):
    return lax.all_to_all(blocks, axes, split_axis=0, concat_axis=0, tiled=True)


def shards(src_feat, tgt_feat, tgt_dual, core_matrix):
    everyone = ("src", "tgt")
    slices, halves = lax.axis_size("src"), lax.axis_size("tgt")
    peers = slices * halves
    own = src_feat.shape[0]
    whole = tgt_feat.shape[0]
    rows, cols = own * slices, whole // slices
    sizes = (rows, whole * halves)
    row_blocks, col_blocks = rows // LANES, cols // LANES

    tgt_pieces = exchanged(tgt_feat.reshape(slices, cols, -1).transpose(0, 2, 1), "src")
    src_pieces = exchanged(jnp.broadcast_to(src_feat.T[None], (peers,) + src_feat.T.shape), everyone)
    order = core_matrix.T
    order = jnp.concatenate([order[2:], order[:2]], axis=0)
    order = jnp.concatenate([order[:, 2:], order[:, 1:2], order[:, :1]], axis=1)
    order = jnp.pad(order, ((0, PAD - RANKS), (0, PAD - RANKS)))

    passed = [((6 * FEAT, rows), BF16), ((PAD - FEAT, rows), F32), ((peers, row_blocks, LANES), F32)]
    left, tgt_left, right, main, tail, part = call(
        functools.partial(first_rows, halves),
        [((PAD, rows), F32), ((PAD, cols), F32), ((cols, DEPTH), BF16)] + passed,
        src_pieces,
        tgt_pieces,
        tgt_dual.reshape(1, whole),
        order,
    )
    for step in range(OUTER):
        last = step == OUTER - 1
        src_dual, dual, core = call(
            functools.partial(col_pass, sizes),
            [
                ((own // LANES, LANES), F32),
                ((col_blocks, LANES), F32),
                ((peers, GROUP + (col_blocks if last else 0), LANES), F32),
            ],
            exchanged(part, everyone),
            main,
            tail,
            right,
            left,
            tgt_left,
            scratch=[pltpu.VMEM((max(WIDE, row_blocks), LANES), F32)],
        )
        core = exchanged(core, everyone)
        if not last:
            (right,) = call(fold_dual, [((cols, DEPTH), BF16)], dual, right)
            main, tail, part = call(later_rows, passed, core, left, right)
    dual, core = call(
        functools.partial(finish, halves),
        [((slices, col_blocks, LANES), F32), ((RANKS, RANKS), F32)],
        core,
    )
    return src_dual.reshape(own), dual.reshape(whole), core


def solution(mesh):
    placed = (
        P(("pairs", "src"), "tgt"),
        P(("pairs", "tgt"), "src"),
        P(("pairs", "tgt")),
        P("pairs", None),
    )
    return jax.shard_map(
        shards,
        mesh=mesh,
        in_specs=placed,
        out_specs=(P(("pairs", "src")), P(("pairs", "tgt")), P("pairs", None)),
        check_vma=False,
    )
```

```python
import functools
import math

import jax
import jax.numpy as jnp
from jax import lax
from jax.experimental import pallas as pl
from jax.experimental.pallas import tpu as pltpu
from jax.sharding import PartitionSpec as P

OUTER = 2
EPSILON = 0.02
SCALE = math.log2(math.e) / EPSILON
HIGH = lax.Precision.HIGHEST
F32 = jnp.float32
BF16 = jnp.bfloat16
FEAT = 32
RANKS = FEAT + 2
PAD = 40
WIDE = 48
DEPTH = 256
LANES = 128
SHIFT = 42
GROUP = 16
CHUNK = 256
VMEM_LIMIT = 20 << 20
NT_DIMS = (((1,), (1,)), ((), ()))


def thirds(values):
    first = values.astype(BF16).astype(F32)
    rest = values - first
    second = rest.astype(BF16).astype(F32)
    third = (rest - second).astype(BF16).astype(F32)
    return first, second, third


def left_order(parts):
    return [parts[0], parts[0], parts[1], parts[0], parts[1], parts[2]]


def right_order(parts):
    return [parts[0], parts[1], parts[0], parts[2], parts[1], parts[0]]


def stacked(rows, count):
    width = rows[0].shape[1]
    index = lax.broadcasted_iota(jnp.int32, (count, width), 0)
    out = jnp.zeros((count, width), F32)
    for k, row in enumerate(rows):
        out = jnp.where(index == k, jnp.broadcast_to(row, (count, width)), out)
    return out


def packed(core_ref, core):
    core_ref[...] = jnp.zeros_like(core_ref)
    core_ref[: core.shape[0], : core.shape[1]] = core
    return (
        core_ref[0:GROUP]
        + pltpu.roll(core_ref[GROUP : 2 * GROUP], SHIFT, 1)
        + pltpu.roll(core_ref[2 * GROUP : 3 * GROUP], 2 * SHIFT, 1)
    )


def unpacked(block):
    pieces = [block, pltpu.roll(block, LANES - SHIFT, 1), pltpu.roll(block, LANES - 2 * SHIFT, 1)]
    whole = jnp.concatenate(pieces, axis=0)
    lane = lax.broadcasted_iota(jnp.int32, whole.shape, 1)
    return jnp.where(lane < RANKS, whole, 0.0)


def row_of(blocks):
    return jnp.concatenate([blocks[k : k + 1] for k in range(blocks.shape[0])], axis=1)


def extras(cross, fixed, ones):
    rows = left_order(thirds(cross)) + list(thirds(fixed))
    if ones:
        rows += [jnp.ones_like(fixed)] * 3
    block = stacked(rows, 16).astype(BF16)
    return jnp.concatenate([block, jnp.zeros((DEPTH - 6 * FEAT - 16, block.shape[1]), BF16)], axis=0)


def row_pass(core, scale, left, right_ref, main_ref, tail_ref, part_ref):
    proj = scale * jnp.dot(core, left, precision=HIGH, preferred_element_type=F32)
    main = jnp.concatenate(left_order(thirds(proj[:FEAT])), axis=0).astype(BF16)
    main_ref[...] = main
    tail_ref[...] = proj[FEAT:PAD]
    weights = jnp.concatenate([main, extras(proj[FEAT + 1 : FEAT + 2], proj[FEAT : FEAT + 1], True)], axis=0)
    count = right_ref.shape[0]
    size = min(CHUNK, count)
    top = total = None
    for start in range(0, count, size):
        logits = jnp.dot(right_ref[start : start + size], weights, preferred_element_type=F32)
        high = jnp.max(logits, axis=0, keepdims=True)
        if top is None:
            top = high
            total = jnp.sum(jnp.exp2(logits - top), axis=0, keepdims=True)
        else:
            new = jnp.maximum(top, high)
            total = total * jnp.exp2(top - new) + jnp.sum(jnp.exp2(logits - new), axis=0, keepdims=True)
            top = new
    part = top + jnp.log2(total)
    peers, blocks, lanes = part_ref.shape
    for k in range(blocks):
        piece = part[:, k * lanes : (k + 1) * lanes]
        for peer in range(peers):
            part_ref[peer, k : k + 1, :] = piece


def first_rows(halves, *refs):
    src_refs, refs = refs[:halves], refs[halves:]
    dual_ref, core_ref, left_ref, tgtl_ref, right_ref, main_ref, tail_ref, part_ref = refs
    feats = FEAT // halves
    mine = lax.axis_index("tgt")
    columns = []
    for k in range(src_refs[0].shape[0]):
        pieces = [ref[k, :feats] for ref in src_refs]
        slots = []
        for t in range(halves):
            slot = pieces[0]
            for shift in range(1, halves):
                slot = jnp.where(lax.rem(t + shift, halves) == mine, pieces[shift], slot)
            slots.append(slot)
        columns.append(jnp.concatenate(slots, axis=0))
    src = jnp.concatenate(columns, axis=1)
    squares = jnp.sum(src * src, axis=0, keepdims=True)
    left_ref[0:FEAT] = -2.0 * src
    left_ref[FEAT:PAD] = stacked([jnp.ones_like(squares), squares], PAD - FEAT)

    all_ref = src_refs[0]
    blocks = all_ref.shape[0]
    depth = FEAT // blocks
    count = tgtl_ref.shape[1]
    for k in range(blocks):
        for j in range(count // LANES):
            piece = all_ref[k, feats + j * depth : feats + (j + 1) * depth]
            tgtl_ref[k * depth : (k + 1) * depth, j * LANES : (j + 1) * LANES] = piece
    tgt = tgtl_ref[0:FEAT]
    norms = jnp.sum(tgt * tgt, axis=0, keepdims=True)
    tgtl_ref[0:FEAT] = -2.0 * tgt
    tgtl_ref[FEAT:PAD] = stacked([norms, jnp.ones_like(norms)], PAD - FEAT)
    start = pl.multiple_of(lax.axis_index("src") * count, LANES)
    dual = SCALE * dual_ref[:, pl.ds(start, count)]
    rows = right_order(thirds(norms)) + [jnp.ones_like(norms)] * 3 + list(thirds(dual))
    tail = jnp.concatenate([stacked(rows, 16), jnp.zeros((DEPTH - 6 * FEAT - 16, count), F32)], axis=0)
    right = jnp.concatenate(right_order(thirds(tgt)) + [tail], axis=0)
    right_ref[...] = right.T.astype(BF16)
    row_pass(core_ref[...], -SCALE, left_ref[...], right_ref, main_ref, tail_ref, part_ref)


def later_rows(core_ref, left_ref, right_ref, main_ref, tail_ref, part_ref):
    core = unpacked(jnp.sum(core_ref[...], axis=0))
    row_pass(core[:PAD, :PAD], 2.0 * SCALE, left_ref[...], right_ref, main_ref, tail_ref, part_ref)


def fold_dual(dual_ref, right_ref, out_ref):
    out_ref[...] = right_ref[...]
    for k in range(dual_ref.shape[0]):
        dual = jnp.broadcast_to(dual_ref[k : k + 1], (LANES, LANES)).T
        parts = thirds(dual)
        old = right_ref[k * LANES : (k + 1) * LANES, LANES:].astype(F32)
        lane = lax.broadcasted_iota(jnp.int32, old.shape, 1) - (6 * FEAT + 9 - LANES)
        for t in range(3):
            old = jnp.where(lane == t, parts[t], old)
        out_ref[k * LANES : (k + 1) * LANES, LANES:] = old.astype(BF16)


def col_pass(sizes, part_ref, main_ref, tail_ref, right_ref, left_ref, tgtl_ref, own_ref, dual_ref, out_ref, pack_ref):
    src_total, tgt_total = sizes
    parts = part_ref[...]
    top = jnp.max(parts, axis=0)
    summed = top + jnp.log2(jnp.sum(jnp.exp2(parts - top[None]), axis=0))
    src_dual = -math.log2(src_total) - summed
    own_rows = own_ref.shape[0]
    pack_ref[0 : src_dual.shape[0]] = src_dual
    own_ref[...] = pack_ref[pl.ds(lax.axis_index("src") * own_rows, own_rows)] * (1.0 / SCALE)

    tail = extras(tail_ref[1:2], tail_ref[0:1] + row_of(src_dual), False)
    weights = jnp.concatenate([main_ref[...], tail], axis=0)
    src = -0.5 * left_ref[0:FEAT]
    squares = left_ref[FEAT + 1 : FEAT + 2]
    ones = left_ref[FEAT : FEAT + 1]
    feats = thirds(src)
    norms = thirds(squares)
    factors = jnp.concatenate(
        [feats[0], stacked([norms[0], ones], GROUP), feats[1], stacked([norms[1]], GROUP)], axis=0
    ).astype(BF16)
    count = right_ref.shape[0]
    size = min(CHUNK, count)
    row = lax.broadcasted_iota(jnp.int32, (LANES, LANES), 0)
    eye = row == lax.broadcasted_iota(jnp.int32, (LANES, LANES), 1)
    core = jnp.zeros((PAD, WIDE), F32)
    peers = out_ref.shape[0]
    for start in range(0, count, size):
        logits = jnp.dot(right_ref[start : start + size], weights, preferred_element_type=F32)
        high = jnp.max(logits, axis=1, keepdims=True)
        weight = jnp.exp2(logits - high)
        coarse = weight.astype(BF16)
        fine = (weight - coarse.astype(F32)).astype(BF16)
        both = lax.dot_general(factors, coarse, NT_DIMS, preferred_element_type=F32)
        rest = lax.dot_general(factors[:WIDE], fine, NT_DIMS, preferred_element_type=F32)
        moments = both[:WIDE] + both[WIDE:] + rest
        total = moments[FEAT + 1 : FEAT + 2]
        tops = []
        for k in range(0, size, LANES):
            block = jnp.broadcast_to(high[k : k + LANES], (LANES, LANES))
            tops.append(jnp.sum(jnp.where(eye, block, 0.0), axis=0, keepdims=True))
        tops = jnp.concatenate(tops, axis=1)
        dual = -math.log2(tgt_total) - (tops + jnp.log2(total))
        for k in range(0, size, LANES):
            dual_ref[(start + k) // LANES : (start + k) // LANES + 1] = dual[:, k : k + LANES]
        moments = moments * ((1.0 / tgt_total) / total)
        core = core + lax.dot_general(
            tgtl_ref[:, start : start + size], moments, NT_DIMS, precision=HIGH, preferred_element_type=F32
        )
    block = packed(pack_ref, core)
    for peer in range(peers):
        out_ref[peer, 0:GROUP] = block
    if out_ref.shape[1] > GROUP:
        for peer in range(peers):
            out_ref[peer, GROUP:] = dual_ref[...]


def finish(halves, in_ref, dual_ref, core_ref):
    half = lax.axis_index("tgt")
    for k in range(dual_ref.shape[0]):
        dual_ref[k] = in_ref[k * halves + half, GROUP:] * (1.0 / SCALE)
    core = unpacked(jnp.sum(in_ref[:, 0:GROUP], axis=0))
    core = jnp.concatenate([core[FEAT:RANKS], core[:FEAT], jnp.zeros((LANES - RANKS, LANES), F32)], axis=0)
    lane = lax.broadcasted_iota(jnp.int32, core.shape, 1)
    moved = pltpu.roll(core, 2, 1)
    moved = jnp.where(lane == 0, pltpu.roll(core, LANES - FEAT - 1, 1), moved)
    moved = jnp.where(lane == 1, pltpu.roll(core, LANES - FEAT + 1, 1), moved)
    core_ref[...] = -2.0 * moved.T[:RANKS, :RANKS]


def call(body, outs, *args, scratch=()):
    spec = pl.BlockSpec(memory_space=pltpu.VMEM)
    return pl.pallas_call(
        body,
        out_shape=[jax.ShapeDtypeStruct(shape, dtype) for shape, dtype in outs],
        in_specs=[spec] * len(args),
        out_specs=[spec] * len(outs),
        scratch_shapes=scratch,
        compiler_params=pltpu.CompilerParams(vmem_limit_bytes=VMEM_LIMIT),
    )(*args)


def exchanged(blocks, axes):
    return lax.all_to_all(blocks, axes, split_axis=0, concat_axis=0, tiled=True)


def shards(src_feat, tgt_feat, tgt_dual, core_matrix):
    everyone = ("src", "tgt")
    slices, halves = lax.axis_size("src"), lax.axis_size("tgt")
    peers = slices * halves
    own = src_feat.shape[0]
    whole = tgt_feat.shape[0]
    rows, cols = own * slices, whole // slices
    sizes = (rows, whole * halves)
    row_blocks, col_blocks = rows // LANES, cols // LANES

    feats = src_feat.shape[1]
    tgt_pieces = tgt_feat.reshape(slices, col_blocks, LANES, -1).transpose(0, 1, 3, 2).reshape(slices, -1, LANES)
    src_pieces = jnp.broadcast_to(src_feat.T[None], (slices, feats, own))
    pieces = exchanged(jnp.concatenate([src_pieces, tgt_pieces], axis=1), "src")
    others = []
    for shift in range(1, halves):
        ring = [(k, (k + shift) % halves) for k in range(halves)]
        others.append(lax.ppermute(pieces[:, :feats], "tgt", ring))
    order = core_matrix.T
    order = jnp.concatenate([order[2:], order[:2]], axis=0)
    order = jnp.concatenate([order[:, 2:], order[:, 1:2], order[:, :1]], axis=1)
    order = jnp.pad(order, ((0, PAD - RANKS), (0, PAD - RANKS)))

    passed = [((6 * FEAT, rows), BF16), ((PAD - FEAT, rows), F32), ((peers, row_blocks, LANES), F32)]
    left, tgt_left, right, main, tail, part = call(
        functools.partial(first_rows, halves),
        [((PAD, rows), F32), ((PAD, cols), F32), ((cols, DEPTH), BF16)] + passed,
        pieces,
        *others,
        tgt_dual.reshape(1, whole),
        order,
    )
    for step in range(OUTER):
        last = step == OUTER - 1
        src_dual, dual, core = call(
            functools.partial(col_pass, sizes),
            [
                ((own // LANES, LANES), F32),
                ((col_blocks, LANES), F32),
                ((peers, GROUP + (col_blocks if last else 0), LANES), F32),
            ],
            exchanged(part, everyone),
            main,
            tail,
            right,
            left,
            tgt_left,
            scratch=[pltpu.VMEM((max(WIDE, row_blocks), LANES), F32)],
        )
        core = exchanged(core, everyone)
        if not last:
            (right,) = call(fold_dual, [((cols, DEPTH), BF16)], dual, right)
            main, tail, part = call(later_rows, passed, core, left, right)
    dual, core = call(
        functools.partial(finish, halves),
        [((slices, col_blocks, LANES), F32), ((RANKS, RANKS), F32)],
        core,
    )
    return src_dual.reshape(own), dual.reshape(whole), core


def solution(mesh):
    placed = (
        P(("pairs", "src"), "tgt"),
        P(("pairs", "tgt"), "src"),
        P(("pairs", "tgt")),
        P("pairs", None),
    )
    return jax.shard_map(
        shards,
        mesh=mesh,
        in_specs=placed,
        out_specs=(P(("pairs", "src")), P(("pairs", "tgt")), P("pairs", None)),
        check_vma=False,
    )
```

```python
import functools
import math

import jax
import jax.numpy as jnp
from jax import lax
from jax.experimental import pallas as pl
from jax.experimental.pallas import tpu as pltpu
from jax.sharding import PartitionSpec as P

OUTER = 2
EPSILON = 0.02
SCALE = math.log2(math.e) / EPSILON
HIGH = lax.Precision.HIGHEST
F32 = jnp.float32
BF16 = jnp.bfloat16
FEAT = 32
RANKS = FEAT + 2
PAD = 40
WIDE = 48
DEPTH = 256
LANES = 128
DUAL_AT = 6 * FEAT + 9 - LANES
SHIFT = 42
GROUP = 16
THIRD = 12
ROWS = 4
UNITS = THIRD // ROWS
CHUNK = 256
COL_CHUNK = 512
VMEM_LIMIT = 20 << 20
NT_DIMS = (((1,), (1,)), ((), ()))


def thirds(values):
    first = values.astype(BF16).astype(F32)
    rest = values - first
    second = rest.astype(BF16).astype(F32)
    third = (rest - second).astype(BF16).astype(F32)
    return first, second, third


def halves_of(values):
    first = values.astype(BF16).astype(F32)
    return first, values - first


def left_order(parts):
    return [parts[0], parts[0], parts[1], parts[0], parts[1], parts[2]]


def right_order(parts):
    return [parts[0], parts[1], parts[0], parts[2], parts[1], parts[0]]


def stacked(rows, count):
    width = rows[0].shape[1]
    index = lax.broadcasted_iota(jnp.int32, (count, width), 0)
    out = jnp.zeros((count, width), F32)
    for k, row in enumerate(rows):
        out = jnp.where(index == k, jnp.broadcast_to(row, (count, width)), out)
    return out


def packed(core_ref, core):
    core_ref[...] = jnp.zeros_like(core_ref)
    core_ref[: core.shape[0], : core.shape[1]] = core
    units = []
    for unit in range(UNITS):
        at = unit * ROWS
        block = core_ref[at : at + ROWS]
        for k in range(1, 3):
            block = block + pltpu.roll(core_ref[k * THIRD + at : k * THIRD + at + ROWS], k * SHIFT, 1)
        units.append(block)
    return units


def unpacked(in_ref, core_ref):
    for unit in range(UNITS):
        block = jnp.sum(in_ref[:, unit], axis=0)
        for k in range(3):
            at = k * THIRD + unit * ROWS
            core_ref[at : at + ROWS] = pltpu.roll(block, LANES - k * SHIFT, 1) if k else block
    whole = core_ref[0 : 3 * THIRD]
    lane = lax.broadcasted_iota(jnp.int32, whole.shape, 1)
    return jnp.where(lane < RANKS, whole, 0.0)


def row_of(blocks):
    return jnp.concatenate([blocks[k : k + 1] for k in range(blocks.shape[0])], axis=1)


def extras(cross, fixed, ones):
    rows = left_order(thirds(cross)) + list(thirds(fixed))
    if ones:
        rows += [jnp.ones_like(fixed)] * 3
    block = stacked(rows, 16).astype(BF16)
    return jnp.concatenate([block, jnp.zeros((DEPTH - 6 * FEAT - 16, block.shape[1]), BF16)], axis=0)


def product(right_ref, rest_ref, start, size, weights):
    rows = pl.ds(start, size)
    return jnp.dot(
        jnp.concatenate([right_ref[rows], rest_ref[rows]], axis=1), weights, preferred_element_type=F32
    )


def row_pass(core, scale, left, right_ref, rest_ref, main_ref, tail_ref, part_ref):
    proj = scale * jnp.dot(core, left, precision=HIGH, preferred_element_type=F32)
    if proj.shape[0] < PAD:
        proj = jnp.concatenate([proj, jnp.zeros((PAD - proj.shape[0], proj.shape[1]), F32)], axis=0)
    main = jnp.concatenate(left_order(thirds(proj[:FEAT])), axis=0).astype(BF16)
    main_ref[...] = main
    tail_ref[...] = proj[FEAT:PAD]
    weights = jnp.concatenate([main, extras(proj[FEAT + 1 : FEAT + 2], proj[FEAT : FEAT + 1], True)], axis=0)
    count = right_ref.shape[0]
    size = min(CHUNK, count)
    top = total = None
    for start in range(0, count, size):
        logits = product(right_ref, rest_ref, start, size, weights)
        high = jnp.max(logits, axis=0, keepdims=True)
        if top is None:
            top = high
            total = jnp.sum(jnp.exp2(logits - top), axis=0, keepdims=True)
        else:
            new = jnp.maximum(top, high)
            total = total * jnp.exp2(top - new) + jnp.sum(jnp.exp2(logits - new), axis=0, keepdims=True)
            top = new
    part = top + jnp.log2(total)
    peers, blocks, lanes = part_ref.shape
    for k in range(blocks):
        piece = part[:, k * lanes : (k + 1) * lanes]
        for peer in range(peers):
            part_ref[peer, k : k + 1, :] = piece


def targets(all_ref, dual_ref, tgtl_ref, right_ref, rest_ref):
    count = tgtl_ref.shape[1]
    blocks = all_ref.shape[0]
    depth = FEAT // blocks
    first = all_ref.shape[1] - depth * count // LANES
    for k in range(blocks):
        for j in range(count // LANES):
            piece = all_ref[k, first + j * depth : first + (j + 1) * depth]
            tgtl_ref[k * depth : (k + 1) * depth, j * LANES : (j + 1) * LANES] = piece
    tgt = tgtl_ref[0:FEAT]
    norms = jnp.sum(tgt * tgt, axis=0, keepdims=True)
    tgtl_ref[0:FEAT] = -2.0 * tgt
    tgtl_ref[FEAT:PAD] = stacked([norms, jnp.ones_like(norms)], PAD - FEAT)
    start = pl.multiple_of(lax.axis_index("src") * count, LANES)
    dual = SCALE * dual_ref[:, pl.ds(start, count)]
    rows = right_order(thirds(norms)) + [jnp.ones_like(norms)] * 3 + list(thirds(dual))
    tail = jnp.concatenate([stacked(rows, 16), jnp.zeros((DEPTH - 6 * FEAT - 16, count), F32)], axis=0)
    right = jnp.concatenate(right_order(thirds(tgt)) + [tail], axis=0)
    right_ref[...] = right[:LANES].T.astype(BF16)
    rest_ref[...] = right[LANES:].T.astype(BF16)


def first_rows(halves, *refs):
    src_refs, refs = refs[:halves], refs[halves:]
    core_ref, right_ref, rest_ref, left_ref, main_ref, tail_ref, part_ref = refs
    feats = FEAT // halves
    mine = lax.axis_index("tgt")
    columns = []
    for k in range(src_refs[0].shape[0]):
        pieces = [ref[k, :feats] for ref in src_refs]
        slots = []
        for t in range(halves):
            slot = pieces[0]
            for shift in range(1, halves):
                slot = jnp.where((t + shift) % halves == mine, pieces[shift], slot)
            slots.append(slot)
        columns.append(jnp.concatenate(slots, axis=0))
    src = jnp.concatenate(columns, axis=1)
    squares = jnp.sum(src * src, axis=0, keepdims=True)
    left_ref[0:FEAT] = -2.0 * src
    left_ref[FEAT:PAD] = stacked([jnp.ones_like(squares), squares], PAD - FEAT)
    row_pass(core_ref[...], -SCALE, left_ref[...], right_ref, rest_ref, main_ref, tail_ref, part_ref)


def later_rows(core_ref, left_ref, right_ref, rest_ref, main_ref, tail_ref, part_ref, pack_ref):
    core = unpacked(core_ref, pack_ref)
    row_pass(core[:RANKS, :PAD], 2.0 * SCALE, left_ref[...], right_ref, rest_ref, main_ref, tail_ref, part_ref)


def col_pass(sizes, part_ref, main_ref, tail_ref, right_ref, rest_ref, left_ref, tgtl_ref, own_ref, dual_ref, out_ref, *refs):
    *later_ref, pack_ref, moment_ref, top_ref, turned_ref = refs
    src_total, tgt_total = sizes
    parts = part_ref[...]
    top = jnp.max(parts, axis=0)
    summed = top + jnp.log2(jnp.sum(jnp.exp2(parts - top[None]), axis=0))
    src_dual = -math.log2(src_total) - summed
    own_rows = own_ref.shape[0]
    pack_ref[0 : src_dual.shape[0]] = src_dual
    own_ref[...] = pack_ref[pl.ds(lax.axis_index("src") * own_rows, own_rows)] * (1.0 / SCALE)

    tail = extras(tail_ref[1:2], tail_ref[0:1] + row_of(src_dual), False)
    weights = jnp.concatenate([main_ref[...], tail], axis=0)
    src = -0.5 * left_ref[0:FEAT]
    squares = left_ref[FEAT + 1 : FEAT + 2]
    ones = left_ref[FEAT : FEAT + 1]
    feats = thirds(src)
    norms = thirds(squares)
    factors = jnp.concatenate(
        [feats[0], stacked([norms[0], ones], GROUP), feats[1], stacked([norms[1]], GROUP)], axis=0
    ).astype(BF16)
    count = right_ref.shape[0]
    size = min(COL_CHUNK, count)
    row = lax.broadcasted_iota(jnp.int32, (LANES, LANES), 0)
    eye = row == lax.broadcasted_iota(jnp.int32, (LANES, LANES), 1)
    peers = out_ref.shape[0]
    starts = range(0, count, size)
    upcoming = product(right_ref, rest_ref, 0, size, weights)
    for start in starts:
        logits = upcoming
        if start + size < count:
            upcoming = product(right_ref, rest_ref, start + size, size, weights)
        high = jnp.max(logits, axis=1, keepdims=True)
        weight = jnp.exp2(logits - high)
        coarse = weight.astype(BF16)
        fine = (weight - coarse.astype(F32)).astype(BF16)
        both = lax.dot_general(factors, coarse, NT_DIMS, preferred_element_type=F32)
        rest = lax.dot_general(factors[:WIDE], fine, NT_DIMS, preferred_element_type=F32)
        moment_ref[:, start : start + size] = both[:WIDE] + both[WIDE:] + rest
        for k in range(0, size, LANES):
            block = jnp.broadcast_to(high[k : k + LANES], (LANES, LANES))
            top_ref[:, start + k : start + k + LANES] = jnp.sum(jnp.where(eye, block, 0.0), axis=0, keepdims=True)
    total = moment_ref[FEAT + 1 : FEAT + 2]
    dual = -math.log2(tgt_total) - (top_ref[...] + jnp.log2(total))
    for k in range(0, count, LANES):
        dual_ref[k // LANES : k // LANES + 1] = dual[:, k : k + LANES]
    moments = halves_of(moment_ref[...] * ((1.0 / tgt_total) / total))
    lifted = jnp.concatenate(halves_of(tgtl_ref[...]), axis=0).astype(BF16)
    both = lax.dot_general(lifted, moments[0].astype(BF16), NT_DIMS, preferred_element_type=F32)
    rest = lax.dot_general(lifted[:PAD], moments[1].astype(BF16), NT_DIMS, preferred_element_type=F32)
    core = both[:PAD] + both[PAD:] + rest
    for unit, block in enumerate(packed(pack_ref, core)):
        for peer in range(peers):
            out_ref[peer, unit] = block
    for unit in range(UNITS, out_ref.shape[1]):
        at = (unit - UNITS) * ROWS
        here = min(ROWS, dual_ref.shape[0] - at)
        for peer in range(peers):
            out_ref[peer, unit, 0:here] = dual_ref[at : at + here]
    if not later_ref:
        return
    parts = thirds(dual)
    turned_ref[...] = jnp.zeros_like(turned_ref)
    lane = lax.broadcasted_iota(jnp.int32, (LANES, LANES), 1)
    inside = jnp.logical_and(lane >= DUAL_AT, lane < DUAL_AT + 3)
    for k in range(0, count, LANES):
        for t in range(3):
            turned_ref[DUAL_AT + t : DUAL_AT + t + 1] = parts[t][:, k : k + LANES]
        old = rest_ref[k : k + LANES].astype(F32)
        later_ref[0][k : k + LANES] = jnp.where(inside, turned_ref[...].T, old).astype(BF16)


def finish(halves, in_ref, dual_ref, core_ref, pack_ref):
    half = lax.axis_index("tgt")
    for k in range(dual_ref.shape[0]):
        for unit in range(UNITS, in_ref.shape[1]):
            at = (unit - UNITS) * ROWS
            here = min(ROWS, dual_ref.shape[1] - at)
            dual_ref[k, at : at + here] = in_ref[k * halves + half, unit, 0:here] * (1.0 / SCALE)
    core = unpacked(in_ref, pack_ref)
    core = jnp.concatenate([core[FEAT:RANKS], core[:FEAT], jnp.zeros((LANES - RANKS, LANES), F32)], axis=0)
    lane = lax.broadcasted_iota(jnp.int32, core.shape, 1)
    moved = pltpu.roll(core, 2, 1)
    moved = jnp.where(lane == 0, pltpu.roll(core, LANES - FEAT - 1, 1), moved)
    moved = jnp.where(lane == 1, pltpu.roll(core, LANES - FEAT + 1, 1), moved)
    core_ref[...] = -2.0 * moved.T[:RANKS, :RANKS]


def call(body, outs, *args, scratch=(), flags=None, cycles=1000):
    spec = pl.BlockSpec(memory_space=pltpu.VMEM)
    return pl.pallas_call(
        body,
        out_shape=[jax.ShapeDtypeStruct(shape, dtype) for shape, dtype in outs],
        in_specs=[spec] * len(args),
        out_specs=[spec] * len(outs),
        scratch_shapes=scratch,
        cost_estimate=pl.CostEstimate(flops=cycles * 100000, bytes_accessed=cycles * 1000, transcendentals=0),
        compiler_params=pltpu.CompilerParams(vmem_limit_bytes=VMEM_LIMIT, flags=flags or {}),
    )(*args)


def exchanged(blocks, axes):
    return lax.all_to_all(blocks, axes, split_axis=0, concat_axis=0, tiled=True)


def shards(src_feat, tgt_feat, tgt_dual, core_matrix):
    everyone = ("src", "tgt")
    slices, halves = lax.axis_size("src"), lax.axis_size("tgt")
    peers = slices * halves
    own = src_feat.shape[0]
    whole = tgt_feat.shape[0]
    rows, cols = own * slices, whole // slices
    sizes = (rows, whole * halves)
    row_blocks, col_blocks = rows // LANES, cols // LANES

    feats = src_feat.shape[1]
    tgt_pieces = tgt_feat.reshape(slices, col_blocks, LANES, -1).transpose(0, 1, 3, 2).reshape(slices, -1, LANES)
    src_pieces = jnp.broadcast_to(src_feat.T[None], (slices, feats, own))
    pieces = exchanged(jnp.concatenate([src_pieces, tgt_pieces], axis=1), "src")
    others = []
    for shift in range(1, halves):
        ring = [(k, (k + shift) % halves) for k in range(halves)]
        others.append(lax.ppermute(pieces[:, :feats], "tgt", ring))
    order = core_matrix.T
    order = jnp.concatenate([order[2:], order[:2]], axis=0)
    order = jnp.concatenate([order[:, 2:], order[:, 1:2], order[:, :1]], axis=1)
    order = jnp.pad(order, ((0, PAD - RANKS), (0, PAD - RANKS)))

    passed = [((6 * FEAT, rows), BF16), ((PAD - FEAT, rows), F32), ((peers, row_blocks, LANES), F32)]
    pack = pltpu.VMEM((max(WIDE, row_blocks), LANES), F32)
    tgt_left, right, rest = call(
        targets,
        [((PAD, cols), F32), ((cols, LANES), BF16), ((cols, LANES), BF16)],
        pieces,
        tgt_dual.reshape(1, whole),
    )
    left, main, tail, part = call(
        functools.partial(first_rows, halves), [((PAD, rows), F32)] + passed, pieces, *others, order, right, rest
    )
    for step in range(OUTER):
        last = step == OUTER - 1
        units = UNITS + (pl.cdiv(col_blocks, ROWS) if last else 0)
        src_dual, dual, core, *folded = call(
            functools.partial(col_pass, sizes),
            [
                ((own // LANES, LANES), F32),
                ((col_blocks, LANES), F32),
                ((peers, units, ROWS, LANES), F32),
            ]
            + ([] if last else [((cols, LANES), BF16)]),
            exchanged(part, everyone),
            main,
            tail,
            right,
            rest,
            left,
            tgt_left,
            scratch=[
                pack,
                pltpu.VMEM((WIDE, cols), F32),
                pltpu.VMEM((1, cols), F32),
                pltpu.VMEM((LANES, LANES), F32),
            ],
        )
        core = exchanged(core, everyone)
        if not last:
            main, tail, part = call(later_rows, passed, core, left, right, *folded, scratch=[pack])
    dual, core = call(
        functools.partial(finish, halves),
        [((slices, col_blocks, LANES), F32), ((RANKS, RANKS), F32)],
        core,
        scratch=[pack],
    )
    return src_dual.reshape(own), dual.reshape(whole), core


def solution(mesh):
    placed = (
        P(("pairs", "src"), "tgt"),
        P(("pairs", "tgt"), "src"),
        P(("pairs", "tgt")),
        P("pairs", None),
    )
    return jax.shard_map(
        shards,
        mesh=mesh,
        in_specs=placed,
        out_specs=(P(("pairs", "src")), P(("pairs", "tgt")), P("pairs", None)),
        check_vma=False,
    )
```
